32 devices in a mesh: row: 4 (over z), col: 4 (over x, core), chol: 2 (over y).
Axes of the slice: x: 2, y: 2, z: 4, core: 2. Of those that a mesh axis runs over, the one named last changes fastest.
Arguments:
- left_vectors: bfloat16 [64, 4608, 1536], P(None, ('col', 'chol'), 'row'), may hold values from -0.75 to 0.75
- right_vectors: bfloat16 [16, 4608, 1536], P(None, ('col', 'chol'), 'row'), may hold values from -0.0234375 to 0.0234375
- amplitudes: bfloat16 [8, 16, 64], replicated, may hold values from -6 to 6
Outputs:
- ladder: float32 [8, 1536, 1536], P('chol', 'row', 'col')
The draws below stay inside these ranges and needn't reach their ends.
All inputs are finite; a program needn't handle non-finite values.
Results may differ from the reference program's by a relative error of at most 0.0029.
Values may be sent and summed in bfloat16 or wider, within the bound.
No kernel may reach another device: no remote copies, remote signals or barrier semaphores. Data moves between devices by JAX's collectives and lax.ppermute only.
A program may use at most 256 MiB of HBM per device.

```python
import jax
import jax.numpy as jnp
from jax import lax

V = 1536
NVEC = 4608
CB = 64
DB = 16
IJ = 8


def level_of(own_key, shape, pieces, smallest, high):
    def one(dim, blocks):
        steps = jax.random.uniform(jax.random.fold_in(jax.random.fold_in(own_key, 6), dim), (blocks,), jnp.float32, smallest / len(pieces), high / len(pieces))
        return jnp.repeat(jnp.exp(steps), shape[dim] // blocks).reshape((-1,) + (1,) * (len(shape) - dim - 1))

    gain = one(*pieces[0])
    for cut in pieces[1:]:
        gain = gain * one(*cut)
    return gain


def centred(stream_key, dims, width, most, pieces=(), dtype=jnp.bfloat16):
    level = level_of(stream_key, dims, pieces, -0.22, 0.18) if pieces else 1.0
    entries = jax.random.normal(stream_key, dims, jnp.float32) * width * level
    return jnp.minimum(jnp.maximum(entries, -most), most).astype(dtype)


def setup_inputs(seed: int = 0) -> dict:
    streams_of = jax.random.split(jax.random.key(seed), 4)
    return {
        "left_vectors": centred(streams_of[0], (CB, NVEC, V), CB ** -0.5, 0.75, ((1, 8), (2, 4))),
        "right_vectors": centred(streams_of[1], (DB, NVEC, V), (NVEC * DB) ** -0.5, 0.0234375, ((1, 8), (2, 4))),
        "amplitudes": centred(streams_of[2], (IJ, DB, CB), 1.0, 6.0),
    }


def reference(left_vectors, right_vectors, amplitudes):
    c_block = left_vectors.shape[0]
    width_a = left_vectors.shape[2]
    left_flat = left_vectors.reshape(c_block, -1)
    right_flat = right_vectors.reshape(-1, right_vectors.shape[2])

    def one_pair(amp_rows):
        halved = jnp.dot(amp_rows, left_flat, preferred_element_type=jnp.float32).astype(jnp.bfloat16)
        halved = halved.reshape(-1, width_a)
        return lax.dot_general(halved, right_flat, (((0,), (0,)), ((), ())), preferred_element_type=jnp.float32)

    return lax.map(one_pair, amplitudes)
```

```python
import jax
import jax.numpy as jnp
from jax import lax
from jax.experimental import pallas as pl
from jax.sharding import PartitionSpec as P


LANES = 128


def half_kernel(amp_ref, left_ref, out_ref):
    pairs, block, d_block, _ = out_ref.shape
    amp = amp_ref[...]
    for p in range(block):
        res = jnp.dot(amp, left_ref[p], preferred_element_type=jnp.float32).astype(out_ref.dtype)
        for i in range(pairs):
            out_ref[i, p] = res[i * d_block:(i + 1) * d_block]


def halve(amplitudes, left_t):
    pairs, d_block, c_block = amplitudes.shape
    vectors, _, width = left_t.shape
    block = next(b for b in (16, 12, 8, 6, 4, 3, 2, 1) if vectors % b == 0)
    return pl.pallas_call(
        half_kernel,
        grid=(vectors // block,),
        in_specs=[
            pl.BlockSpec((pairs * d_block, c_block), lambda p: (0, 0)),
            pl.BlockSpec((block, c_block, width), lambda p: (p, 0, 0)),
        ],
        out_specs=pl.BlockSpec((pairs, block, d_block, width), lambda p: (0, p, 0, 0)),
        out_shape=jax.ShapeDtypeStruct((pairs, vectors, d_block, width), jnp.bfloat16),
        cost_estimate=pl.CostEstimate(
            flops=2 * pairs * d_block * c_block * vectors * width,
            bytes_accessed=2 * vectors * width * (c_block + pairs * d_block),
            transcendentals=0,
        ),
        name="halve",
    )(amplitudes.reshape(pairs * d_block, c_block), left_t)


def product(halved, block):
    pairs, vectors, d_block, width = halved.shape
    return jnp.einsum(
        "ika,kb->iab",
        halved.reshape(pairs, vectors * d_block, width),
        block.reshape(vectors * d_block, block.shape[2]),
        preferred_element_type=jnp.float32,
    )


class Reducer:
    def __init__(self):
        self.rows, self.cols, self.chols = (lax.axis_size(n) for n in ("row", "col", "chol"))
        self.duo = 2 if self.cols % 2 == 0 else 1
        self.col, self.chol = lax.axis_index("col"), lax.axis_index("chol")
        self.core = self.col % self.duo

    def swap(self, value):
        if self.duo == 1:
            return value
        return lax.ppermute(value, "col", [(q, q ^ 1) for q in range(self.cols)])

    def flat(self, row, col, chol):
        return (row * self.cols + col) * self.chols + chol

    def reduce(self, block, owner):
        pairs, width_a, width_b = block.shape
        half = width_a // self.duo
        mine = lax.dynamic_slice_in_dim(block, self.core * half, half, 1)
        if self.duo == 2:
            other = lax.dynamic_slice_in_dim(block, (1 - self.core) * half, half, 1)
            mine = mine + self.swap(other)
        mine = mine.reshape(self.chols, pairs // self.chols, half, width_b)
        low = mine.astype(jnp.bfloat16)
        groups = self.cols // self.duo
        total = None
        for dc in range(self.chols):
            part = lax.dynamic_index_in_dim(low, (self.chol - dc) % self.chols, 0, False)
            for dg in range(groups):
                if not (dc or dg):
                    continue
                perm = []
                for r in range(self.rows):
                    g = owner(r) // self.duo
                    for c in range(self.duo):
                        for h in range(self.chols):
                            perm.append((
                                self.flat(r, (g + dg) % groups * self.duo + c, (h + dc) % self.chols),
                                self.flat(r, g * self.duo + c, h)))
                got = lax.ppermute(part, ("row", "col", "chol"), perm).astype(jnp.float32)
                total = got if total is None else total + got
        here = lax.dynamic_index_in_dim(mine, self.chol, 0, False)
        total = here if total is None else here + total
        to = sum(jnp.where(lax.axis_index("row") == r, owner(r), 0) for r in range(self.rows))
        keep = jnp.where(to == self.col, total, 0.0)
        give = jnp.where(to == (self.col ^ 1 if self.duo == 2 else -1), total, 0.0)
        return keep, give

    def finish(self, keep, give):
        if self.duo == 1:
            return keep
        got = self.swap(give)
        first = self.core == 0
        return jnp.concatenate([jnp.where(first, keep, got), jnp.where(first, got, keep)], axis=1)


def gathered(left_vectors, right_vectors, amplitudes):
    columns = lax.axis_size("col")
    right_t = lax.all_gather(right_vectors, "row", axis=2, tiled=True).transpose(1, 0, 2)
    halved = halve(amplitudes, left_vectors.transpose(1, 0, 2))
    total = product(halved, right_t)
    pairs, width_a, width_b = total.shape
    total = total.reshape(pairs, width_a, columns, width_b // columns).transpose(2, 0, 1, 3)
    total = total.reshape(columns * pairs, width_a, width_b // columns)
    return lax.psum_scatter(total, ("col", "chol"), scatter_dimension=0, tiled=True)


def shards(left_vectors, right_vectors, amplitudes):
    return ladder_of(left_vectors, right_vectors, amplitudes)


def ladder_of(left_vectors, right_vectors, amplitudes):
    row = lax.axis_index("row")
    mate_pairs = ((0, 1), (1, 0), (2, 3), (3, 2))
    cross_pairs = ((1, 2), (2, 1))
    out_pairs = ((1, 0), (2, 3))
    inner = (row == 1) | (row == 2)
    owners = (lambda r: r, lambda r: r ^ 1, lambda r: 1 if r >= 2 else 2, lambda r: 0 if r >= 2 else 3)
    red = Reducer()

    def send(value, perm):
        return lax.ppermute(value, "row", perm)

    def reduce(block, owner):
        return red.reduce(block, owner)

    own = right_vectors.transpose(1, 0, 2)
    mate = send(own, mate_pairs)
    cross_in = send(own, cross_pairs)
    halved = halve(amplitudes, left_vectors.transpose(1, 0, 2))
    cross_out = send(cross_in, out_pairs)
    width_b = own.shape[2]
    cuts = [slice(0, 2 * LANES), slice(2 * LANES, width_b)]
    far_in = [send(mate[:, :, cut], cross_pairs) for cut in cuts]

    y_own = product(halved, own)
    y_mate = product(halved, mate)
    totals = [reduce(y_own, owners[0]), reduce(y_mate, owners[1])]
    far_out = [send(part, out_pairs) for part in far_in]
    y_cross = product(halved, jnp.where(inner, cross_in, cross_out))
    totals.append(reduce(y_cross, owners[2]))
    far = []
    for far_i, far_o in zip(far_in, far_out):
        y_far = product(halved, jnp.where(inner, far_i, far_o))
        far.append(reduce(y_far, owners[3]))
    keep, give = (sum(t[s] for t in totals) for s in range(2))
    outs = []
    for cut, (k, g) in zip(cuts, far):
        outs.append(red.finish(keep[:, :, cut] + k, give[:, :, cut] + g))
    return jnp.concatenate(outs, axis=2)


def solution(mesh):
    lined = mesh.shape["row"] == 4
    return jax.shard_map(
        shards if lined else gathered,
        mesh=mesh,
        in_specs=(P(None, ("col", "chol"), "row"), P(None, ("col", "chol"), "row"), P()),
        out_specs=P("chol", "row", "col"),
        check_vma=False,
    )
```
